32 devices in a mesh: leaf: 8 (over z, x), band: 4 (over y, core).
Axes of the slice: x: 2, y: 2, z: 4, core: 2. Of those that a mesh axis runs over, the one named last changes fastest.
Arguments:
- excitation: float32 [16, 8, 65536], P(None, None, 'leaf'), may hold values from -6 to 6
- freq_index: int32 [4], P('band'), may hold values from 1 to 3
- elem_order: int32 [8, 8192], P('leaf'), may hold values from 0 to 8191, each once within a row
- level_factors: bfloat16 [4, 8, 9, 2, 2, 128, 128], P('band', 'leaf'), may hold values from -1 to 1
- image_weights: bfloat16 [4, 2, 64, 65536], P('band', None, None, 'leaf'), may hold values from -0.5 to 0.5
- coupling: bfloat16 [4, 2, 128, 128], P('band'), may hold values from -0.375 to 0.375
- reflectivity: bfloat16 [65536, 128], P('leaf'), may hold values from -4 to 4
- clip_level: int32 [16], replicated, may hold values from 0 to 8
Outputs:
- retransmit: float32 [16, 8, 65536], P(None, None, 'leaf')
The draws below stay inside these ranges and needn't reach their ends.
Inputs may be any that keep to these rules, and one draw needn't show every extreme that they name: `elem_order`: each row holds every number from 0 to 8191 once.
All inputs are finite; a program needn't handle non-finite values.
Results may differ from the reference program's by a relative error of at most 0.014.
Values sent between devices are 32-bit elements; how exact they have to be, the bound alone decides.
A program may use at most 64 MiB of HBM per device.

```python
import math
import jax
import jax.numpy as jnp
from jax import lax

ELEMENTS = 65536
IMAGE = 8388608
RANK = 128
LEVELS = 9
SAMPLES = 8
ITERS = 2
SHOTS = 16
BANDS = 4
E_DEV = 8192
BOXES = 64
IMG_DEV = 8192
N_LEAF = 8


def draw_level_factors(key, part):
    shape = (BANDS, N_LEAF, LEVELS, 2, 2, RANK, RANK)
    base = jax.random.normal(key, shape, jnp.float32) * (4.0 * RANK) ** (-0.5)
    base = jnp.clip(base, -6.0 * (4.0 * RANK) ** (-0.5), 6.0 * (4.0 * RANK) ** (-0.5))
    rise = jnp.log(3.0)
    leaf_pos = jnp.arange(N_LEAF, dtype=jnp.float32) / (N_LEAF - 1)
    leaf_scale = jnp.exp(rise * leaf_pos) / jnp.exp(rise * 0.5)
    level_pick = (jnp.arange(LEVELS) == 0).astype(jnp.float32)
    factor = 1.0 + (leaf_scale[:, None] - 1.0) * level_pick[None, :]
    scaled = base * factor[None, :, :, None, None, None, None]
    scaled = jnp.clip(scaled, -0.99, 0.99)
    return scaled.astype(jnp.bfloat16)


def plant(array, rng, low, largest):
    longest = array.shape.index(max(array.shape))
    spots = []
    for shift in (0, 1):
        where = [jax.random.randint(jax.random.fold_in(rng, axis), (), 0, length) for axis, length in enumerate(array.shape)]
        where[longest] = (where[longest] + shift) % array.shape[longest]
        spots.append(tuple(where))
    return array.at[spots[0]].set(low).at[spots[1]].set(largest)


def shard_levels(rng, dims, split, smallest, largest):
    level = 1.0
    for axis_at, blocks in split:
        heights = jax.random.uniform(jax.random.fold_in(jax.random.fold_in(rng, 6), axis_at), (blocks,), jnp.float32, smallest / len(split), largest / len(split))
        level = level * jnp.repeat(jnp.exp(heights), dims[axis_at] // blocks).reshape((-1,) + (1,) * (len(dims) - 1 - axis_at))
    return level


def scatter_about(key, extent, width, limit, shards=(), kind=jnp.bfloat16):
    values = jax.random.normal(key, extent, jnp.float32) * width
    if len(shards) > 0:
        values = shard_levels(key, extent, shards, -0.22, 0.18) * values
    return jnp.clip(values, min=-limit, max=limit).astype(kind)


def setup_inputs(seed: int = 0) -> dict:
    key_list = jax.random.split(jax.random.key(seed), 9)
    return {
        "excitation": scatter_about(key_list[0], (SHOTS, SAMPLES, ELEMENTS), 1.0, 6.0, ((2, 8),), jnp.float32),
        "freq_index": plant(jax.random.randint(key_list[1], (BANDS,), 1, SAMPLES // 2), jax.random.fold_in(key_list[1], 1), 1, (SAMPLES // 2) - 1).astype(jnp.int32),
        "elem_order": jax.vmap(lambda own: jax.random.permutation(own, E_DEV))(jax.random.split(key_list[2], N_LEAF)).reshape((N_LEAF, E_DEV)).astype(jnp.int32),
        "level_factors": draw_level_factors(jax.random.fold_in(key_list[8], 71), 0),
        "image_weights": scatter_about(key_list[4], (BANDS, 2, BOXES, IMAGE // RANK), (2 * BOXES) ** -0.5, 0.5, ((0, 4), (3, 8))),
        "coupling": scatter_about(key_list[5], (BANDS, 2, RANK, RANK), (2 * RANK) ** -0.5, 0.375, ((0, 4),)),
        "reflectivity": scatter_about(key_list[6], (IMAGE // RANK, RANK), 1.0, 4.0, ((0, 8),)),
        "clip_level": plant(jax.random.randint(key_list[7], (SHOTS,), 0, 9), jax.random.fold_in(key_list[7], 1), 0, 8).astype(jnp.int32),
    }


def block_form(real_part, imag_part):
    top_rows = jnp.concatenate([real_part, imag_part], axis=-1)
    bottom_rows = jnp.concatenate([-imag_part, real_part], axis=-1)
    return jnp.concatenate([top_rows, bottom_rows], axis=-2)

def flip_pairs(values, axis_num, bit_num):
    moved = jnp.moveaxis(values, axis_num, 0)
    lead_count = moved.shape[0]
    half_span = 1 << bit_num
    folded = moved.reshape((lead_count // (2 * half_span), 2, half_span) + moved.shape[1:])
    folded = folded[:, ::-1]
    return jnp.moveaxis(folded.reshape(moved.shape), 0, axis_num)

def image_pass(coeffs, weights, reflect, couple_mat):
    turned = jnp.concatenate([-coeffs[..., RANK:], coeffs[..., :RANK]], axis=-1)
    stacked = jnp.concatenate([coeffs, turned], axis=0).reshape(2 * BOXES, SHOTS * 2 * RANK)
    flat_weights = weights.reshape(2 * BOXES, IMG_DEV)
    image_field = lax.dot_general(flat_weights, stacked, (((0,), (0,)), ((), ())), preferred_element_type=jnp.float32)
    image_field = image_field.reshape(IMG_DEV, SHOTS, 2 * RANK)
    reflect_pair = jnp.concatenate([reflect, reflect], axis=-1).astype(jnp.float32)[:, None, :]
    scaled = (reflect_pair * image_field).astype(jnp.bfloat16)
    coupled = jnp.dot(scaled.reshape(IMG_DEV * SHOTS, 2 * RANK), couple_mat, preferred_element_type=jnp.float32)
    coupled = coupled.reshape(IMG_DEV, SHOTS, 2 * RANK)
    echo_field = (reflect_pair * (image_field + coupled)).astype(jnp.bfloat16)
    turned_back = jnp.concatenate([echo_field[..., RANK:], -echo_field[..., :RANK]], axis=-1)
    summed = jnp.dot(weights[0], echo_field.reshape(IMG_DEV, SHOTS * 2 * RANK), preferred_element_type=jnp.float32)
    summed = summed + jnp.dot(weights[1], turned_back.reshape(IMG_DEV, SHOTS * 2 * RANK), preferred_element_type=jnp.float32)
    return summed.reshape(BOXES, SHOTS, 2 * RANK)

def reference(excitation, freq_index, elem_order, level_factors, image_weights, coupling, reflectivity, clip_level):
    highest = lax.Precision.HIGHEST
    local_levels = BOXES.bit_length() - 1
    self_mats = block_form(level_factors[:, :, :, 0, 0], level_factors[:, :, :, 0, 1])
    cross_mats = block_form(level_factors[:, :, :, 1, 0], level_factors[:, :, :, 1, 1])
    global_perm = (jnp.arange(N_LEAF, dtype=jnp.int32)[:, None] * E_DEV + elem_order).reshape(-1).astype(jnp.int32)
    inverse = jnp.argsort(global_perm).astype(jnp.int32)
    reflect_leaf = reflectivity.reshape(N_LEAF, IMG_DEV, RANK)
    time_steps = jnp.arange(SAMPLES, dtype=jnp.float32)
    clip_scale = (4.0 + clip_level.astype(jnp.float32)) / 10.0
    signal = excitation
    for iteration in range(ITERS):
        summed = jnp.zeros((SHOTS, SAMPLES, ELEMENTS), jnp.float32)
        for band_idx in range(BANDS):
            phase_angle = 2.0 * math.pi / SAMPLES * freq_index[band_idx].astype(jnp.float32) * time_steps
            cosine = jnp.cos(phase_angle)
            sine_table = jnp.sin(phase_angle)
            spec_real = lax.optimization_barrier(jnp.sum(signal * cosine[None, :, None], axis=1))[:, global_perm]
            spec_imag = (-lax.optimization_barrier(jnp.sum(signal * sine_table[None, :, None], axis=1)))[:, global_perm]
            joined = jnp.concatenate([spec_real.reshape(SHOTS, N_LEAF, BOXES, RANK), spec_imag.reshape(SHOTS, N_LEAF, BOXES, RANK)], axis=-1)
            coeffs = joined.transpose(1, 2, 0, 3).astype(jnp.float32)
            band_self = self_mats[band_idx].astype(jnp.float32)
            band_cross = cross_mats[band_idx].astype(jnp.float32)
            for level_idx in range(LEVELS):
                if level_idx < local_levels:
                    partner = flip_pairs(coeffs, 1, level_idx)
                else:
                    partner = flip_pairs(coeffs, 0, level_idx - local_levels)
                coeffs = jnp.einsum('lbsk,lkm->lbsm', coeffs, band_self[:, level_idx], precision=highest) + jnp.einsum('lbsk,lkm->lbsm', partner, band_cross[:, level_idx], precision=highest)
            weights_leaf = image_weights[band_idx].reshape(2, BOXES, N_LEAF, IMG_DEV).transpose(2, 0, 1, 3)
            couple_mat = block_form(coupling[band_idx, 0], coupling[band_idx, 1])
            coeffs = lax.map(lambda items: image_pass(items[0], items[1], items[2], couple_mat), (coeffs.astype(jnp.bfloat16), weights_leaf, reflect_leaf))
            for level_idx in reversed(range(LEVELS)):
                outgoing = jnp.einsum('lbsm,lkm->lbsk', coeffs, band_cross[:, level_idx], precision=highest)
                if level_idx < local_levels:
                    incoming = flip_pairs(outgoing, 1, level_idx)
                else:
                    incoming = flip_pairs(outgoing, 0, level_idx - local_levels)
                coeffs = jnp.einsum('lbsm,lkm->lbsk', coeffs, band_self[:, level_idx], precision=highest) + incoming
            real_part = coeffs[..., :RANK].transpose(2, 0, 1, 3).reshape(SHOTS, ELEMENTS)[:, inverse]
            imag_part = coeffs[..., RANK:].transpose(2, 0, 1, 3).reshape(SHOTS, ELEMENTS)[:, inverse]
            summed = summed + real_part[:, None, :] * cosine[None, :, None] - imag_part[:, None, :] * sine_table[None, :, None]
        energy = lax.optimization_barrier(jnp.sum(summed * summed, axis=(1, 2)))
        root_mean = jnp.sqrt(energy / (SAMPLES * ELEMENTS) + 1e-06)
        clip_amp = (clip_scale * root_mean)[:, None, None]
        signal = jnp.clip(summed, -clip_amp, clip_amp) / clip_amp
    return signal
```

```python
import functools
import math

import jax
import jax.numpy as jnp
from jax import lax
from jax.experimental import pallas as pl
from jax.experimental.pallas import tpu as pltpu
from jax.sharding import PartitionSpec as P

ITERS = 2
F32 = jnp.float32
BF16 = jnp.bfloat16
SUB = 8


def call(body, outs, args, flops, grid=None, in_specs=None, out_specs=None, scratch=()):
    vmem = pl.BlockSpec(memory_space=pltpu.VMEM)
    size = sum(math.prod(a.shape) * a.dtype.itemsize for a in list(args) + list(outs))
    kw = {}
    if grid is not None:
        kw["grid"] = grid
    return pl.pallas_call(
        body,
        out_shape=outs,
        in_specs=in_specs or [vmem] * len(args),
        out_specs=out_specs or [vmem] * len(outs),
        scratch_shapes=scratch,
        cost_estimate=pl.CostEstimate(flops=flops, bytes_accessed=size, transcendentals=0),
        **kw,
    )(*args)


def sds(shape, dtype=F32):
    return jax.ShapeDtypeStruct(shape, dtype)


def swap(value, axis, bit):
    mask = 1 << bit
    pairs = [(src, src ^ mask) for src in range(lax.axis_size(axis))]
    return lax.ppermute(value, axis, pairs)


def block_form(real_part, imag_part):
    top = jnp.concatenate([real_part, imag_part], axis=-1)
    bottom = jnp.concatenate([-imag_part, real_part], axis=-1)
    return jnp.concatenate([top, bottom], axis=-2)


def mm(a, b):
    return jnp.dot(a, b, preferred_element_type=F32)


def split(x):
    hi = x.astype(BF16)
    return hi, (x - hi.astype(F32)).astype(BF16)


def dot2(x, m):
    hi, lo = split(x)
    return mm(hi, m) + mm(lo, m)


def dot3(x, mh, ml):
    hi, lo = split(x)
    return mm(hi, mh) + mm(lo, mh) + mm(hi, ml)


def prep_local(fac, hi, lo, hit, lot):
    f = fac[0].astype(F32)
    a = block_form(f[0, 0], f[0, 1])
    b = block_form(f[1, 0], f[1, 1])
    for i, m in enumerate((a + b, a - b)):
        hi[0, i], lo[0, i] = split(m)
        hit[0, i], lot[0, i] = split(m.T)


def prep_cross(fac, mats, matst):
    f = fac[0].astype(F32)
    for i in range(2):
        m = block_form(f[i, 0], f[i, 1])
        mats[0, i] = m.astype(BF16)
        matst[0, i] = m.T.astype(BF16)


def prepare(factors, local_levels):
    levels, _, _, rank, _ = factors.shape
    width = 2 * rank

    def spec(n):
        return pl.BlockSpec((1, 2, n, n), lambda i: (i, 0, 0, 0))

    fspec = pl.BlockSpec((1, 2, 2, rank, rank), lambda i: (i, 0, 0, 0, 0))
    loc = call(
        prep_local,
        [sds((local_levels, 2, width, width), BF16)] * 4,
        [factors[:local_levels]],
        1 << 20,
        grid=(local_levels,),
        in_specs=[fspec],
        out_specs=[spec(width)] * 4,
    )
    n_cross = levels - local_levels
    cro = call(
        prep_cross,
        [sds((n_cross, 2, width, width), BF16)] * 2,
        [factors[local_levels:]],
        1 << 20,
        grid=(n_cross,),
        in_specs=[fspec],
        out_specs=[spec(width)] * 2,
    )
    return loc, cro


def hadamard(v, bits):
    count, rows, lanes = v.shape
    for bit in range(bits):
        half = 1 << bit
        v = v.reshape(count // (2 * half), 2, half, rows, lanes)
        a, b = v[:, 0], v[:, 1]
        v = jnp.stack([a + b, a - b], axis=1).reshape(count, rows, lanes)
    return v


def local_levels_apply(v, hi, lo, order, bits):
    count, rows, lanes = v.shape
    v = hadamard(v, bits)
    for level in order:
        half = 1 << level
        v = v.reshape(count // (2 * half), 2, half, rows, lanes)
        parts = []
        for i in range(2):
            piece = v[:, i].reshape(count // 2 * rows, lanes)
            out = dot3(piece, hi[level, i], lo[level, i])
            parts.append(out.reshape(count // (2 * half), half, rows, lanes))
        v = jnp.stack(parts, axis=1).reshape(count, rows, lanes)
    return hadamard(v, bits) * (1.0 / count)


def rows_to_boxes(spec, boxes, rank):
    out = []
    for c in range(boxes):
        cols = spec[:, c * rank : (c + 1) * rank]
        out.append(jnp.concatenate([cols[:SUB], cols[SUB:]], axis=1)[None])
    return jnp.concatenate(out, axis=0)


def forward_tail(spec, hi, lo, outs, boxes, rank, bits):
    v = rows_to_boxes(spec, boxes, rank)
    v = local_levels_apply(v, hi, lo, range(bits), bits)
    flat = v.reshape(boxes * SUB, 2 * rank)
    part = boxes * SUB // len(outs)
    for i, out in enumerate(outs):
        out[...] = flat[i * part : (i + 1) * part]


def permute_rows(src, idx, dst):
    rows = src.shape[0]
    blocks = src.shape[1] // 128

    def step(j, carry):
        at = idx[pl.ds(j, 1), :]
        hi_part = jnp.broadcast_to(at // 128, (8, 128))
        lo_part = jnp.broadcast_to(at % 128, (8, 128))
        accs = [jnp.zeros((8, 128), F32) for _ in range(rows // 8)]
        for c in range(blocks):
            hit = hi_part == c
            for r in range(rows // 8):
                val = src[r * 8 : (r + 1) * 8, c * 128 : (c + 1) * 128]
                got = jnp.take_along_axis(val, lo_part, axis=1)
                accs[r] = jnp.where(hit, got, accs[r])
        at_col = pl.multiple_of(j * 128, 128)
        for r in range(rows // 8):
            dst[r * 8 : (r + 1) * 8, pl.ds(at_col, 128)] = accs[r]
        return carry

    lax.fori_loop(0, blocks, step, 0)


def first_spec(exc, idx, mat, out, tmp):
    hi, lo = split(mat[...])
    chunk = math.gcd(exc.shape[1], 1024)

    def step(i, carry):
        at = pl.multiple_of(i * chunk, chunk)
        xh, xl = split(exc[:, pl.ds(at, chunk)])
        tmp[:, pl.ds(at, chunk)] = mm(hi, xh) + mm(hi, xl) + mm(lo, xh)
        return carry

    lax.fori_loop(0, exc.shape[1] // chunk, step, 0)
    permute_rows(tmp, idx, out)


def start_levels(spec, hi, lo, *outs, boxes, rank, bits):
    forward_tail(spec[...], hi, lo, outs, boxes, rank, bits)


def band_sum(backs, tables, t):
    total = None
    for k, back in enumerate(backs):
        term = back[:SUB, :] * tables[k, 0, t] - back[SUB:, :] * tables[k, 1, t]
        total = term if total is None else total + term
    return total


def energy_body(tables, *refs, samples):
    backs, out = refs[:-1], refs[-1]
    total = jnp.zeros((SUB, backs[0].shape[1]), F32)
    for t in range(samples):
        val = band_sum(backs, tables, t)
        total = total + val * val
    out[...] = jnp.broadcast_to(jnp.sum(total, axis=1, keepdims=True), out.shape)


def amp_of(energy, scale, count):
    root = jnp.sqrt(energy[:, :1] / count + 1e-06)
    return scale[:, :1] * root


def next_levels(tables, own, energy, scale, hi, lo, *refs, samples, count, boxes, rank, bits, bands):
    backs, outs = refs[:bands], refs[bands:]
    amp = amp_of(energy, scale, count)
    inv = 1.0 / amp
    re = jnp.zeros((SUB, backs[0].shape[1]), F32)
    im = jnp.zeros((SUB, backs[0].shape[1]), F32)
    for t in range(samples):
        sig = jnp.clip(band_sum(backs, tables, t), -amp, amp) * inv
        re = re + sig * own[0, t]
        im = im - sig * own[1, t]
    forward_tail(jnp.concatenate([re, im], axis=0), hi, lo, outs, boxes, rank, bits)


def finish(tables, *refs, samples, count, halves, bands):
    energies = refs[:halves]
    scales = refs[halves : 2 * halves]
    backs = refs[2 * halves : 2 * halves + halves * bands]
    out = refs[-1]
    for h in range(halves):
        amp = amp_of(energies[h], scales[h], count)
        inv = 1.0 / amp
        for t in range(samples):
            sig = band_sum(backs[h * bands : (h + 1) * bands], tables, t)
            sig = jnp.clip(sig, -amp, amp) * inv
            out[t, h * SUB : (h + 1) * SUB, :] = sig


def cross_body(x, p, m, out):
    out[...] = dot2(x[...], m[0]) + dot2(p[...], m[1])


def back_first(x, m, out):
    out[...] = dot2(x[...], m[1])


def back_mid(x, inc, m, nxt, keep, out):
    v = dot2(x[...], m[0]) + inc[...]
    keep[...] = v
    out[...] = dot2(v, nxt[1])


def back_last(*refs, parts, boxes, rank, bits, final):
    xs, incs = refs[:parts], refs[parts : 2 * parts]
    m, hi, lo = refs[2 * parts : 2 * parts + 3]
    rest = refs[2 * parts + 3 :]
    v = jnp.concatenate(
        [dot2(xs[i][...], m[0]) + incs[i][...] for i in range(parts)], axis=0
    ).reshape(boxes, SUB, 2 * rank)
    v = local_levels_apply(v, hi, lo, reversed(range(bits)), bits)
    if final:
        idx, out, tmp = rest
    else:
        (out,) = rest
        tmp = out
    for c in range(boxes):
        cols = slice(c * rank, (c + 1) * rank)
        tmp[:SUB, cols] = v[c, :, :rank]
        tmp[SUB:, cols] = v[c, :, rank:]
    if final:
        permute_rows(tmp, idx, out)


def image_body(*refs, parts, boxes, rank):
    xs = refs[:parts]
    wt, w, rho, couple = refs[parts : parts + 4]
    outs = refs[parts + 4 : 2 * parts + 4]
    st, acc, pre, pim = refs[2 * parts + 4 :]
    step = pl.program_id(0)
    width = 2 * rank
    per = boxes // parts

    @pl.when(step == 0)
    def _():
        for i in range(parts):
            pre[...] = xs[i][:, :rank]
            pim[...] = xs[i][:, rank:]
            for s in range(SUB):
                re = pre[pl.ds(s, per, stride=SUB), :].astype(BF16)
                im = pim[pl.ds(s, per, stride=SUB), :].astype(BF16)
                at = s * width
                st[i * per : (i + 1) * per, at : at + rank] = re
                st[i * per : (i + 1) * per, at + rank : at + width] = im
                st[boxes + i * per : boxes + (i + 1) * per, at : at + rank] = -im
                st[boxes + i * per : boxes + (i + 1) * per, at + rank : at + width] = re
        acc[...] = jnp.zeros_like(acc)

    r = rho[...].astype(F32)
    pair = jnp.concatenate([r, r], axis=1)
    k = couple[...]
    wtb = wt[...]
    wb = w[...]
    for s in range(SUB):
        cols = slice(s * width, (s + 1) * width)
        field = mm(wtb, st[:, cols])
        scaled = (pair * field).astype(BF16)
        echo = (pair * (field + mm(scaled, k))).astype(BF16)
        acc[:, cols] += mm(wb, echo)

    @pl.when(step == pl.num_programs(0) - 1)
    def _():
        for i in range(parts):
            top = slice(i * per, (i + 1) * per)
            low = slice(boxes + i * per, boxes + (i + 1) * per)
            for s in range(SUB):
                at = s * width
                a_re, a_im = acc[top, at : at + rank], acc[top, at + rank : at + width]
                b_re, b_im = acc[low, at : at + rank], acc[low, at + rank : at + width]
                pre[pl.ds(s, per, stride=SUB), :] = a_re + b_im
                pim[pl.ds(s, per, stride=SUB), :] = a_im - b_re
            outs[i][:, :rank] = pre[...]
            outs[i][:, rank:] = pim[...]


def image_pass(xs, wt, w, rho, couple):
    parts = len(xs)
    points, double = wt.shape
    boxes = double // 2
    rank = rho.shape[1]
    width = 2 * rank
    blk = math.gcd(points, 1024)
    whole = pl.BlockSpec(memory_space=pltpu.VMEM)
    return call(
        functools.partial(image_body, parts=parts, boxes=boxes, rank=rank),
        [sds(xs[0].shape)] * parts,
        [*xs, wt, w, rho, couple],
        points * SUB * width * 2 * (2 * double + width),
        grid=(points // blk,),
        in_specs=[whole] * parts
        + [
            pl.BlockSpec((blk, double), lambda i: (i, 0)),
            pl.BlockSpec((double, blk), lambda i: (0, i)),
            pl.BlockSpec((blk, rank), lambda i: (i, 0)),
            whole,
        ],
        out_specs=[whole] * parts,
        scratch=[
            pltpu.VMEM((double, SUB * width), BF16),
            pltpu.VMEM((double, SUB * width), F32),
            pltpu.VMEM((xs[0].shape[0], rank), F32),
            pltpu.VMEM((xs[0].shape[0], rank), F32),
        ],
    )


def on_device(
    excitation,
    freq_index,
    elem_order,
    level_factors,
    image_weights,
    coupling,
    reflectivity,
    clip_level,
):
    shots, samples, elems = excitation.shape
    rank = coupling.shape[-1]
    boxes = elems // rank
    bits = boxes.bit_length() - 1
    levels = level_factors.shape[2]
    n_cross = levels - bits
    leafs = lax.axis_size("leaf")
    bands = lax.axis_size("band")
    band_bits = bands.bit_length() - 1
    halves = shots // SUB
    parts = 2
    width = 2 * rank
    rows = boxes * SUB
    count = float(samples * elems * leafs)

    (hi, lo, hit, lot), (cross, crosst) = prepare(level_factors[0, 0], bits)
    w = image_weights[0].reshape(2 * boxes, image_weights.shape[3])
    wt = w.T
    couple = block_form(coupling[0, 0], coupling[0, 1])
    order = elem_order[0]
    inverse = jnp.argsort(order)
    idx = order.reshape(boxes, rank)
    inv_idx = inverse.astype(jnp.int32).reshape(boxes, rank)

    steps = jnp.arange(samples, dtype=F32)
    angle = 2.0 * math.pi / samples * freq_index[0].astype(F32) * steps
    own = jnp.stack([jnp.cos(angle), jnp.sin(angle)])
    smem = pl.BlockSpec(memory_space=pltpu.SMEM)
    vmem = pl.BlockSpec(memory_space=pltpu.VMEM)

    def gather_bands(value):
        got = [value]
        for bit in reversed(range(band_bits)):
            got = got + [swap(v, "band", bit) for v in got]
        return got

    tables = jnp.stack(gather_bands(own))
    scale = (4.0 + clip_level.astype(F32)) / 10.0
    scales = [
        jnp.broadcast_to(scale[h * SUB : (h + 1) * SUB, None], (SUB, 128)) for h in range(halves)
    ]

    eye = jnp.eye(SUB, dtype=F32)
    half_mat = jnp.concatenate(
        [
            (eye[:, :, None] * own[0][None, None, :]).reshape(SUB, SUB * samples),
            (eye[:, :, None] * -own[1][None, None, :]).reshape(SUB, SUB * samples),
        ],
        axis=0,
    )
    mat = jnp.kron(jnp.eye(halves, dtype=F32), half_mat)
    spec = call(
        first_spec,
        [sds((shots * 2, elems))],
        [excitation.reshape(shots * samples, elems), idx, mat],
        1 << 24,
        scratch=[pltpu.VMEM((shots * 2, elems), F32)],
    )[0]
    part_out = [sds((rows // parts, width))] * parts
    loc_flops = 6 * rows * width * width * bits
    cr_flops = 8 * rows // parts * width * width
    xs = []
    for h in range(halves):
        xs.append(
            call(
                functools.partial(start_levels, boxes=boxes, rank=rank, bits=bits),
                part_out,
                [spec[h * 2 * SUB : (h + 1) * 2 * SUB], hi, lo],
                loc_flops,
            )
        )
    result = None
    for it in range(ITERS):
        final = it == ITERS - 1
        all_backs, all_energy = [], []
        for h in range(halves):
            x = list(xs[h])
            for l in range(n_cross):
                for i in range(parts):
                    p = swap(x[i], "leaf", l)
                    x[i] = call(cross_body, part_out[:1], [x[i], p, cross[l]], cr_flops)[0]
            x = list(image_pass(x, wt, w, reflectivity, couple))
            sent = [
                call(back_first, part_out[:1], [x[i], crosst[n_cross - 1]], cr_flops // 2)[0]
                for i in range(parts)
            ]
            for l in reversed(range(n_cross)):
                inc = [swap(sent[i], "leaf", l) for i in range(parts)]
                if l > 0:
                    for i in range(parts):
                        x[i], sent[i] = call(
                            back_mid,
                            part_out[:1] * 2,
                            [x[i], inc[i], crosst[l], crosst[l - 1]],
                            cr_flops,
                        )
            back = call(
                functools.partial(
                    back_last, parts=parts, boxes=boxes, rank=rank, bits=bits, final=final
                ),
                [sds((2 * SUB, elems))],
                [*x, *inc, crosst[0], hit, lot] + ([inv_idx] if final else []),
                loc_flops,
                scratch=[pltpu.VMEM((2 * SUB, elems), F32)] if final else [],
            )[0]
            backs = gather_bands(back)
            energy = call(
                functools.partial(energy_body, samples=samples),
                [sds((SUB, 128))],
                [tables, *backs],
                1 << 22,
                in_specs=[smem] + [vmem] * bands,
            )[0]
            for bit in range(leafs.bit_length() - 1):
                energy = energy + swap(energy, "leaf", bit)
            all_backs.append(backs)
            all_energy.append(energy)
        if not final:
            xs = [
                call(
                    functools.partial(
                        next_levels,
                        samples=samples,
                        count=count,
                        boxes=boxes,
                        rank=rank,
                        bits=bits,
                        bands=bands,
                    ),
                    part_out,
                    [tables, own, all_energy[h], scales[h], hi, lo, *all_backs[h]],
                    loc_flops,
                    in_specs=[smem, smem] + [vmem] * (4 + bands),
                )
                for h in range(halves)
            ]
        else:
            flat = [b for bs in all_backs for b in bs]
            result = call(
                functools.partial(finish, samples=samples, count=count, halves=halves, bands=bands),
                [sds((samples, shots, elems))],
                [tables, *all_energy, *scales, *flat],
                1 << 24,
                in_specs=[smem] + [vmem] * (2 * halves + len(flat)),
            )[0]
    return result.transpose(1, 0, 2)


def solution(mesh):
    return jax.shard_map(
        on_device,
        mesh=mesh,
        in_specs=(
            P(None, None, "leaf"),
            P("band"),
            P("leaf", None),
            P("band", "leaf", None, None, None, None, None),
            P("band", None, None, "leaf"),
            P("band", None, None, None),
            P("leaf", None),
            P(),
        ),
        out_specs=P(None, None, "leaf"),
        check_vma=False,
    )
```

```python
import functools
import math

import jax
import jax.numpy as jnp
from jax import lax
from jax.experimental import pallas as pl
from jax.experimental.pallas import tpu as pltpu
from jax.sharding import PartitionSpec as P

ITERS = 2
F32 = jnp.float32
BF16 = jnp.bfloat16
SUB = 8
PARTS = 1
SEGS = 2


def call(body, outs, args, flops, grid=None, in_specs=None, out_specs=None, scratch=(), mib=16):
    vmem = pl.BlockSpec(memory_space=pltpu.VMEM)
    size = sum(math.prod(a.shape) * a.dtype.itemsize for a in list(args) + list(outs))
    kw = {}
    if grid is not None:
        kw["grid"] = grid
    return pl.pallas_call(
        body,
        out_shape=outs,
        in_specs=in_specs or [vmem] * len(args),
        out_specs=out_specs or [vmem] * len(outs),
        scratch_shapes=scratch,
        compiler_params=pltpu.CompilerParams(vmem_limit_bytes=mib << 20),
        cost_estimate=pl.CostEstimate(flops=flops, bytes_accessed=size, transcendentals=0),
        **kw,
    )(*args)


def sds(shape, dtype=F32):
    return jax.ShapeDtypeStruct(shape, dtype)


def swap(value, axis, bit):
    mask = 1 << bit
    pairs = [(src, src ^ mask) for src in range(lax.axis_size(axis))]
    return lax.ppermute(value, axis, pairs)


def block_form(real_part, imag_part):
    top = jnp.concatenate([real_part, imag_part], axis=-1)
    bottom = jnp.concatenate([-imag_part, real_part], axis=-1)
    return jnp.concatenate([top, bottom], axis=-2)


def mm(a, b):
    return jnp.dot(a, b, preferred_element_type=F32)


def split(x):
    hi = x.astype(BF16)
    return hi, (x - hi.astype(F32)).astype(BF16)


def dot2(x, m):
    hi, lo = split(x)
    return mm(hi, m) + mm(lo, m)


def dot3(x, mh, ml):
    hi, lo = split(x)
    return mm(hi, mh) + mm(lo, mh) + mm(hi, ml)


def prep_local(fac, hi, lo, hit, lot):
    f = fac[0].astype(F32)
    a = block_form(f[0, 0], f[0, 1])
    b = block_form(f[1, 0], f[1, 1])
    for i, m in enumerate((a + b, a - b)):
        hi[0, i], lo[0, i] = split(m)
        hit[0, i], lot[0, i] = split(m.T)


def prep_cross(fac, mats, matst):
    f = fac[0].astype(F32)
    for i in range(2):
        m = block_form(f[i, 0], f[i, 1])
        mats[0, i] = m.astype(BF16)
        matst[0, i] = m.T.astype(BF16)


def prepare(factors, local_levels):
    levels, _, _, rank, _ = factors.shape
    width = 2 * rank

    def spec(n):
        return pl.BlockSpec((1, 2, n, n), lambda i: (i, 0, 0, 0))

    fspec = pl.BlockSpec((1, 2, 2, rank, rank), lambda i: (i, 0, 0, 0, 0))
    loc = call(
        prep_local,
        [sds((local_levels, 2, width, width), BF16)] * 4,
        [factors[:local_levels]],
        1 << 20,
        grid=(local_levels,),
        in_specs=[fspec],
        out_specs=[spec(width)] * 4,
    )
    n_cross = levels - local_levels
    cro = call(
        prep_cross,
        [sds((n_cross, 2, width, width), BF16)] * 2,
        [factors[local_levels:]],
        1 << 20,
        grid=(n_cross,),
        in_specs=[fspec],
        out_specs=[spec(width)] * 2,
    )
    return loc, cro


def hadamard(v, bits):
    count, rows, lanes = v.shape
    for bit in range(bits):
        half = 1 << bit
        v = v.reshape(count // (2 * half), 2, half, rows, lanes)
        a, b = v[:, 0], v[:, 1]
        v = jnp.stack([a + b, a - b], axis=1).reshape(count, rows, lanes)
    return v


def local_levels_apply(v, hi, lo, order, bits):
    count, rows, lanes = v.shape
    v = hadamard(v, bits)
    for level in order:
        half = 1 << level
        v = v.reshape(count // (2 * half), 2, half, rows, lanes)
        parts = []
        for i in range(2):
            piece = v[:, i].reshape(count // 2 * rows, lanes)
            out = dot3(piece, hi[level, i], lo[level, i])
            parts.append(out.reshape(count // (2 * half), half, rows, lanes))
        v = jnp.stack(parts, axis=1).reshape(count, rows, lanes)
    return hadamard(v, bits) * (1.0 / count)


def rows_to_boxes(spec, boxes, rank):
    out = []
    for c in range(boxes):
        cols = spec[:, c * rank : (c + 1) * rank]
        out.append(jnp.concatenate([cols[:SUB], cols[SUB:]], axis=1)[None])
    return jnp.concatenate(out, axis=0)


def forward_tail(spec, hi, lo, outs, boxes, rank, bits):
    v = rows_to_boxes(spec, boxes, rank)
    v = local_levels_apply(v, hi, lo, range(bits), bits)
    flat = v.reshape(boxes * SUB, 2 * rank)
    part = boxes * SUB // len(outs)
    for i, out in enumerate(outs):
        out[...] = flat[i * part : (i + 1) * part]


def permute_rows(src, idx, dst):
    rows = src.shape[0]
    blocks = src.shape[1] // 128

    def step(j, carry):
        at = idx[pl.ds(j, 1), :]
        hi_part = jnp.broadcast_to(at // 128, (8, 128))
        lo_part = jnp.broadcast_to(at % 128, (8, 128))
        accs = [jnp.zeros((8, 128), F32) for _ in range(rows // 8)]
        for c in range(blocks):
            hit = hi_part == c
            for r in range(rows // 8):
                val = src[r * 8 : (r + 1) * 8, c * 128 : (c + 1) * 128]
                got = jnp.take_along_axis(val, lo_part, axis=1)
                accs[r] = jnp.where(hit, got, accs[r])
        at_col = pl.multiple_of(j * 128, 128)
        for r in range(rows // 8):
            dst[r * 8 : (r + 1) * 8, pl.ds(at_col, 128)] = accs[r]
        return carry

    lax.fori_loop(0, blocks, step, 0)


def first_spec(exc, idx, mat, out, tmp):
    hi, lo = split(mat[...])
    chunk = math.gcd(exc.shape[1], 1024)

    def step(i, carry):
        at = pl.multiple_of(i * chunk, chunk)
        xh, xl = split(exc[:, pl.ds(at, chunk)])
        tmp[:, pl.ds(at, chunk)] = mm(hi, xh) + mm(hi, xl) + mm(lo, xh)
        return carry

    lax.fori_loop(0, exc.shape[1] // chunk, step, 0)
    permute_rows(tmp, idx, out)


def start_levels(spec, hi, lo, *outs, boxes, rank, bits):
    forward_tail(spec[...], hi, lo, outs, boxes, rank, bits)


def band_sum(backs, tables, t):
    total = None
    for k, back in enumerate(backs):
        term = back[:SUB, :] * tables[k, 0, t] - back[SUB:, :] * tables[k, 1, t]
        total = term if total is None else total + term
    return total


def energy_body(tables, *refs, samples):
    backs, out = refs[:-1], refs[-1]
    total = jnp.zeros((SUB, backs[0].shape[1]), F32)
    for t in range(samples):
        val = band_sum(backs, tables, t)
        total = total + val * val
    out[...] = jnp.broadcast_to(jnp.sum(total, axis=1, keepdims=True), out.shape)


def leaf_sum_body(src, out, slots, send, recv, *, n):
    me = lax.axis_index("leaf")

    def peer(d):
        got = me
        for bit in range(n.bit_length() - 1):
            if (d >> bit) & 1:
                got = got + (1 << bit) * (1 - 2 * (me // (1 << bit) % 2))
        return got

    barrier = pltpu.get_barrier_semaphore()
    for d in range(1, n):
        pl.semaphore_signal(
            barrier, inc=1, device_id={"leaf": peer(d)}, device_id_type=pl.DeviceIdType.MESH
        )
    pl.semaphore_wait(barrier, n - 1)
    copies = []
    for d in range(1, n):
        copy = pltpu.make_async_remote_copy(
            src_ref=src,
            dst_ref=slots.at[d],
            send_sem=send.at[d],
            recv_sem=recv.at[d],
            device_id={"leaf": peer(d)},
            device_id_type=pl.DeviceIdType.MESH,
        )
        copy.start()
        copies.append(copy)
    for copy in copies:
        copy.wait()
    total = src[...]
    for d in range(1, n):
        total = total + slots[d]
    out[...] = total


def leaf_sum(value, n, tag):
    vmem = pl.BlockSpec(memory_space=pltpu.VMEM)
    return pl.pallas_call(
        functools.partial(leaf_sum_body, n=n),
        out_shape=sds(value.shape),
        in_specs=[vmem],
        out_specs=vmem,
        scratch_shapes=[
            pltpu.VMEM((n,) + value.shape, F32),
            pltpu.SemaphoreType.DMA((n,)),
            pltpu.SemaphoreType.DMA((n,)),
        ],
        compiler_params=pltpu.CompilerParams(
            collective_id=tag, has_side_effects=True, vmem_limit_bytes=4 << 20
        ),
        cost_estimate=pl.CostEstimate(flops=1 << 20, bytes_accessed=1 << 16, transcendentals=0),
    )(value)


def amp_of(energy, scale, count):
    root = jnp.sqrt(energy[:, :1] / count + 1e-06)
    return scale[:, :1] * root


def next_levels(tables, own, energy, scale, hi, lo, *refs, samples, count, boxes, rank, bits, bands):
    backs, outs = refs[:bands], refs[bands:]
    amp = amp_of(energy, scale, count)
    inv = 1.0 / amp
    re = jnp.zeros((SUB, backs[0].shape[1]), F32)
    im = jnp.zeros((SUB, backs[0].shape[1]), F32)
    for t in range(samples):
        sig = jnp.clip(band_sum(backs, tables, t), -amp, amp) * inv
        re = re + sig * own[0, t]
        im = im - sig * own[1, t]
    forward_tail(jnp.concatenate([re, im], axis=0), hi, lo, outs, boxes, rank, bits)


def finish(tables, *refs, samples, count, halves, bands):
    energies = refs[:halves]
    scales = refs[halves : 2 * halves]
    backs = refs[2 * halves : 2 * halves + halves * bands]
    out = refs[-1]
    for h in range(halves):
        amp = amp_of(energies[h], scales[h], count)
        inv = 1.0 / amp
        for t in range(samples):
            sig = band_sum(backs[h * bands : (h + 1) * bands], tables, t)
            sig = jnp.clip(sig, -amp, amp) * inv
            out[t, h * SUB : (h + 1) * SUB, :] = sig


def cross_body(x, p, m, out):
    out[...] = dot2(x[...], m[0]) + dot2(p[...], m[1])


def back_first(*refs):
    xs, (m, keep, out) = refs[:-3], refs[-3:]
    v = xs[0][...]
    for x in xs[1:]:
        v = v + x[...]
    keep[...] = v
    out[...] = dot2(v, m[1])


def back_mid(x, inc, m, nxt, keep, out):
    v = dot2(x[...], m[0]) + inc[...]
    keep[...] = v
    out[...] = dot2(v, nxt[1])


def back_last(*refs, parts, boxes, rank, bits, final):
    xs, incs = refs[:parts], refs[parts : 2 * parts]
    m, hi, lo = refs[2 * parts : 2 * parts + 3]
    rest = refs[2 * parts + 3 :]
    v = jnp.concatenate(
        [dot2(xs[i][...], m[0]) + incs[i][...] for i in range(parts)], axis=0
    ).reshape(boxes, SUB, 2 * rank)
    v = local_levels_apply(v, hi, lo, reversed(range(bits)), bits)
    if final:
        idx, out, tmp = rest
    else:
        (out,) = rest
        tmp = out
    for c in range(boxes):
        cols = slice(c * rank, (c + 1) * rank)
        tmp[:SUB, cols] = v[c, :, :rank]
        tmp[SUB:, cols] = v[c, :, rank:]
    if final:
        permute_rows(tmp, idx, out)


def image_body(*refs, parts, boxes, rank):
    xs = refs[:parts]
    wt, w, rho, couple = refs[parts : parts + 4]
    outs = refs[parts + 4 : 2 * parts + 4]
    st, acc, pre, pim = refs[2 * parts + 4 :]
    step = pl.program_id(0)
    width = 2 * rank
    per = boxes // parts

    @pl.when(step == 0)
    def _():
        for i in range(parts):
            pre[...] = xs[i][:, :rank]
            pim[...] = xs[i][:, rank:]
            for s in range(SUB):
                re = pre[pl.ds(s, per, stride=SUB), :].astype(BF16)
                im = pim[pl.ds(s, per, stride=SUB), :].astype(BF16)
                at = s * width
                st[i * per : (i + 1) * per, at : at + rank] = re
                st[i * per : (i + 1) * per, at + rank : at + width] = im
                st[boxes + i * per : boxes + (i + 1) * per, at : at + rank] = -im
                st[boxes + i * per : boxes + (i + 1) * per, at + rank : at + width] = re
        acc[...] = jnp.zeros_like(acc)

    r = rho[...].astype(F32)
    pair = jnp.concatenate([r, r], axis=1)
    k = couple[...]
    wtb = wt[...]
    wb = w[...]
    for s in range(SUB):
        cols = slice(s * width, (s + 1) * width)
        field = mm(wtb, st[:, cols])
        scaled = (pair * field).astype(BF16)
        echo = (pair * (field + mm(scaled, k))).astype(BF16)
        acc[:, cols] += mm(wb, echo)

    @pl.when(step == pl.num_programs(0) - 1)
    def _():
        for i in range(parts):
            top = slice(i * per, (i + 1) * per)
            low = slice(boxes + i * per, boxes + (i + 1) * per)
            for s in range(SUB):
                at = s * width
                a_re, a_im = acc[top, at : at + rank], acc[top, at + rank : at + width]
                b_re, b_im = acc[low, at : at + rank], acc[low, at + rank : at + width]
                pre[pl.ds(s, per, stride=SUB), :] = a_re + b_im
                pim[pl.ds(s, per, stride=SUB), :] = a_im - b_re
            outs[i][:, :rank] = pre[...]
            outs[i][:, rank:] = pim[...]


def image_pass(xs, wt, w, rho, couple, seg):
    parts = len(xs)
    points, double = wt.shape
    boxes = double // 2
    rank = rho.shape[1]
    width = 2 * rank
    blk = math.gcd(points // SEGS, 1024)
    steps = points // SEGS // blk
    first = seg * steps
    whole = pl.BlockSpec(memory_space=pltpu.VMEM)
    return call(
        functools.partial(image_body, parts=parts, boxes=boxes, rank=rank),
        [sds(xs[0].shape)] * parts,
        [*xs, wt, w, rho, couple],
        2 * points // SEGS * SUB * width * 2 * (2 * double + width),
        grid=(steps,),
        mib=24,
        in_specs=[whole] * parts
        + [
            pl.BlockSpec((blk, double), lambda i: (i + first, 0)),
            pl.BlockSpec((double, blk), lambda i: (0, i + first)),
            pl.BlockSpec((blk, rank), lambda i: (i + first, 0)),
            whole,
        ],
        out_specs=[whole] * parts,
        scratch=[
            pltpu.VMEM((double, SUB * width), BF16),
            pltpu.VMEM((double, SUB * width), F32),
            pltpu.VMEM((xs[0].shape[0], rank), F32),
            pltpu.VMEM((xs[0].shape[0], rank), F32),
        ],
    )


def on_device(
    excitation,
    freq_index,
    elem_order,
    level_factors,
    image_weights,
    coupling,
    reflectivity,
    clip_level,
):
    shots, samples, elems = excitation.shape
    rank = coupling.shape[-1]
    boxes = elems // rank
    bits = boxes.bit_length() - 1
    levels = level_factors.shape[2]
    n_cross = levels - bits
    leafs = lax.axis_size("leaf")
    bands = lax.axis_size("band")
    band_bits = bands.bit_length() - 1
    halves = shots // SUB
    parts = PARTS
    width = 2 * rank
    rows = boxes * SUB
    count = float(samples * elems * leafs)

    (hi, lo, hit, lot), (cross, crosst) = prepare(level_factors[0, 0], bits)
    w = image_weights[0].reshape(2 * boxes, image_weights.shape[3])
    wt = w.T
    couple = block_form(coupling[0, 0], coupling[0, 1])
    order = elem_order[0]
    inverse = jnp.argsort(order)
    idx = order.reshape(boxes, rank)
    inv_idx = inverse.astype(jnp.int32).reshape(boxes, rank)

    steps = jnp.arange(samples, dtype=F32)
    angle = 2.0 * math.pi / samples * freq_index[0].astype(F32) * steps
    own = jnp.stack([jnp.cos(angle), jnp.sin(angle)])
    smem = pl.BlockSpec(memory_space=pltpu.SMEM)
    vmem = pl.BlockSpec(memory_space=pltpu.VMEM)

    def gather_bands(value):
        got = [value]
        for bit in reversed(range(band_bits)):
            got = got + [swap(v, "band", bit) for v in got]
        return got

    tables = jnp.stack(gather_bands(own))
    scale = (4.0 + clip_level.astype(F32)) / 10.0
    scales = [
        jnp.broadcast_to(scale[h * SUB : (h + 1) * SUB, None], (SUB, 128)) for h in range(halves)
    ]

    eye = jnp.eye(SUB, dtype=F32)
    half_mat = jnp.concatenate(
        [
            (eye[:, :, None] * own[0][None, None, :]).reshape(SUB, SUB * samples),
            (eye[:, :, None] * -own[1][None, None, :]).reshape(SUB, SUB * samples),
        ],
        axis=0,
    )
    flat_exc = excitation.reshape(shots * samples, elems)
    in_rows = SUB * samples
    specs = [
        call(
            first_spec,
            [sds((SUB * 2, elems))],
            [flat_exc, idx, half_mat],
            1 << 33,
            grid=(1,),
            in_specs=[pl.BlockSpec((in_rows, elems), lambda i, h=h: (h, 0)), vmem, vmem],
            scratch=[pltpu.VMEM((SUB * 2, elems), F32)],
            mib=20,
        )[0]
        for h in range(halves)
    ]
    part_out = [sds((rows // parts, width))] * parts
    loc_flops = 6 * rows * width * width * bits
    cr_flops = 8 * rows // parts * width * width
    xs = []
    for h in range(halves):
        xs.append(
            call(
                functools.partial(start_levels, boxes=boxes, rank=rank, bits=bits),
                part_out,
                [specs[h], hi, lo],
                loc_flops,
            )
        )
    result = None
    for it in range(ITERS):
        final = it == ITERS - 1
        all_backs, all_energy = [], []
        for h in range(halves):
            x = list(xs[h])
            for l in range(n_cross):
                for i in range(parts):
                    p = swap(x[i], "leaf", l)
                    x[i] = call(cross_body, part_out[:1], [x[i], p, cross[l]], cr_flops, mib=6)[0]
            segs = [image_pass(x, wt, w, reflectivity, couple, g) for g in range(SEGS)]
            sent = [None] * parts
            for i in range(parts):
                x[i], sent[i] = call(
                    back_first,
                    part_out[:1] * 2,
                    [*[g[i] for g in segs], crosst[n_cross - 1]],
                    cr_flops // 2,
                    mib=6,
                )
            for l in reversed(range(n_cross)):
                inc = [swap(sent[i], "leaf", l) for i in range(parts)]
                if l > 0:
                    for i in range(parts):
                        x[i], sent[i] = call(
                            back_mid,
                            part_out[:1] * 2,
                            [x[i], inc[i], crosst[l], crosst[l - 1]],
                            cr_flops,
                            mib=6,
                        )
            back = call(
                functools.partial(
                    back_last, parts=parts, boxes=boxes, rank=rank, bits=bits, final=final
                ),
                [sds((2 * SUB, elems))],
                [*x, *inc, crosst[0], hit, lot] + ([inv_idx] if final else []),
                loc_flops,
                scratch=[pltpu.VMEM((2 * SUB, elems), F32)] if final else [],
            )[0]
            backs = gather_bands(back)
            energy = call(
                functools.partial(energy_body, samples=samples),
                [sds((SUB, 128))],
                [tables, *backs],
                1 << 22,
                in_specs=[smem] + [vmem] * bands,
            )[0]
            energy = leaf_sum(energy, leafs, it * halves + h)
            all_backs.append(backs)
            all_energy.append(energy)
        if not final:
            xs = [
                call(
                    functools.partial(
                        next_levels,
                        samples=samples,
                        count=count,
                        boxes=boxes,
                        rank=rank,
                        bits=bits,
                        bands=bands,
                    ),
                    part_out,
                    [tables, own, all_energy[h], scales[h], hi, lo, *all_backs[h]],
                    loc_flops,
                    in_specs=[smem, smem] + [vmem] * (4 + bands),
                )
                for h in range(halves)
            ]
        else:
            flat = [b for bs in all_backs for b in bs]
            result = call(
                functools.partial(finish, samples=samples, count=count, halves=halves, bands=bands),
                [sds((samples, shots, elems))],
                [tables, *all_energy, *scales, *flat],
                1 << 24,
                in_specs=[smem] + [vmem] * (2 * halves + len(flat)),
            )[0]
    return result.transpose(1, 0, 2)


def solution(mesh):
    return jax.shard_map(
        on_device,
        mesh=mesh,
        in_specs=(
            P(None, None, "leaf"),
            P("band"),
            P("leaf", None),
            P("band", "leaf", None, None, None, None, None),
            P("band", None, None, "leaf"),
            P("band", None, None, None),
            P("leaf", None),
            P(),
        ),
        out_specs=P(None, None, "leaf"),
        check_vma=False,
    )
```

```python
import functools
import math

import jax
import jax.numpy as jnp
from jax import lax
from jax.experimental import pallas as pl
from jax.experimental.pallas import tpu as pltpu
from jax.sharding import PartitionSpec as P

ITERS = 2
F32 = jnp.float32
BF16 = jnp.bfloat16
SUB = 8
PARTS = 1
SEGS = ((0, 3), (3, 1))


def call(body, outs, args, flops, grid=None, in_specs=None, out_specs=None, scratch=(), mib=16):
    vmem = pl.BlockSpec(memory_space=pltpu.VMEM)
    size = sum(math.prod(a.shape) * a.dtype.itemsize for a in list(args) + list(outs))
    kw = {}
    if grid is not None:
        kw["grid"] = grid
    return pl.pallas_call(
        body,
        out_shape=outs,
        in_specs=in_specs or [vmem] * len(args),
        out_specs=out_specs or [vmem] * len(outs),
        scratch_shapes=scratch,
        compiler_params=pltpu.CompilerParams(vmem_limit_bytes=mib << 20),
        cost_estimate=pl.CostEstimate(flops=flops, bytes_accessed=size, transcendentals=0),
        **kw,
    )(*args)


def sds(shape, dtype=F32):
    return jax.ShapeDtypeStruct(shape, dtype)


def swap(value, axis, bit):
    mask = 1 << bit
    pairs = [(src, src ^ mask) for src in range(lax.axis_size(axis))]
    return lax.ppermute(value, axis, pairs)


def block_form(real_part, imag_part):
    top = jnp.concatenate([real_part, imag_part], axis=-1)
    bottom = jnp.concatenate([-imag_part, real_part], axis=-1)
    return jnp.concatenate([top, bottom], axis=-2)


def mm(a, b):
    return jnp.dot(a, b, preferred_element_type=F32)


def split(x):
    hi = x.astype(BF16)
    return hi, (x - hi.astype(F32)).astype(BF16)


def dot2(x, m):
    hi, lo = split(x)
    return mm(hi, m) + mm(lo, m)


def dot3(x, mh, ml):
    hi, lo = split(x)
    return mm(hi, mh) + mm(lo, mh) + mm(hi, ml)


def prep_local(fac, hi, lo, hit, lot):
    f = fac[0].astype(F32)
    a = block_form(f[0, 0], f[0, 1])
    b = block_form(f[1, 0], f[1, 1])
    for i, m in enumerate((a + b, a - b)):
        hi[0, i], lo[0, i] = split(m)
        hit[0, i], lot[0, i] = split(m.T)


def prep_cross(fac, mats, matst):
    f = fac[0].astype(F32)
    for i in range(2):
        m = block_form(f[i, 0], f[i, 1])
        mats[0, i] = m.astype(BF16)
        matst[0, i] = m.T.astype(BF16)


def prepare(factors, local_levels):
    levels, _, _, rank, _ = factors.shape
    width = 2 * rank

    def spec(n):
        return pl.BlockSpec((1, 2, n, n), lambda i: (i, 0, 0, 0))

    fspec = pl.BlockSpec((1, 2, 2, rank, rank), lambda i: (i, 0, 0, 0, 0))
    loc = call(
        prep_local,
        [sds((local_levels, 2, width, width), BF16)] * 4,
        [factors[:local_levels]],
        1 << 20,
        grid=(local_levels,),
        in_specs=[fspec],
        out_specs=[spec(width)] * 4,
    )
    n_cross = levels - local_levels
    cro = call(
        prep_cross,
        [sds((n_cross, 2, width, width), BF16)] * 2,
        [factors[local_levels:]],
        1 << 20,
        grid=(n_cross,),
        in_specs=[fspec],
        out_specs=[spec(width)] * 2,
    )
    return loc, cro


def hadamard(v, bits):
    count, rows, lanes = v.shape
    for bit in range(bits):
        half = 1 << bit
        v = v.reshape(count // (2 * half), 2, half, rows, lanes)
        a, b = v[:, 0], v[:, 1]
        v = jnp.stack([a + b, a - b], axis=1).reshape(count, rows, lanes)
    return v


def local_levels_apply(v, hi, lo, order, bits):
    count, rows, lanes = v.shape
    v = hadamard(v, bits)
    for level in order:
        half = 1 << level
        v = v.reshape(count // (2 * half), 2, half, rows, lanes)
        parts = []
        for i in range(2):
            piece = v[:, i].reshape(count // 2 * rows, lanes)
            out = dot3(piece, hi[level, i], lo[level, i])
            parts.append(out.reshape(count // (2 * half), half, rows, lanes))
        v = jnp.stack(parts, axis=1).reshape(count, rows, lanes)
    return hadamard(v, bits) * (1.0 / count)


def rows_to_boxes(spec, boxes, rank):
    out = []
    for c in range(boxes):
        cols = spec[:, c * rank : (c + 1) * rank]
        out.append(jnp.concatenate([cols[:SUB], cols[SUB:]], axis=1)[None])
    return jnp.concatenate(out, axis=0)


def forward_tail(spec, hi, lo, outs, boxes, rank, bits):
    v = rows_to_boxes(spec, boxes, rank)
    v = local_levels_apply(v, hi, lo, range(bits), bits)
    flat = v.reshape(boxes * SUB, 2 * rank)
    part = boxes * SUB // len(outs)
    for i, out in enumerate(outs):
        out[...] = flat[i * part : (i + 1) * part]


def permute_rows(src, idx, dst):
    rows = src.shape[0]
    blocks = src.shape[1] // 128

    def step(j, carry):
        at = idx[pl.ds(j, 1), :]
        hi_part = jnp.broadcast_to(at // 128, (8, 128))
        lo_part = jnp.broadcast_to(at % 128, (8, 128))
        accs = [jnp.zeros((8, 128), F32) for _ in range(rows // 8)]
        for c in range(blocks):
            hit = hi_part == c
            for r in range(rows // 8):
                val = src[r * 8 : (r + 1) * 8, c * 128 : (c + 1) * 128]
                got = jnp.take_along_axis(val, lo_part, axis=1)
                accs[r] = jnp.where(hit, got, accs[r])
        at_col = pl.multiple_of(j * 128, 128)
        for r in range(rows // 8):
            dst[r * 8 : (r + 1) * 8, pl.ds(at_col, 128)] = accs[r]
        return carry

    lax.fori_loop(0, blocks, step, 0)


def first_spec(exc, idx, mat, out, tmp):
    hi, lo = split(mat[...])
    chunk = math.gcd(exc.shape[1], 1024)

    def step(i, carry):
        at = pl.multiple_of(i * chunk, chunk)
        xh, xl = split(exc[:, pl.ds(at, chunk)])
        tmp[:, pl.ds(at, chunk)] = mm(hi, xh) + mm(hi, xl) + mm(lo, xh)
        return carry

    lax.fori_loop(0, exc.shape[1] // chunk, step, 0)
    permute_rows(tmp, idx, out)


def start_levels(spec, hi, lo, *outs, boxes, rank, bits):
    forward_tail(spec[...], hi, lo, outs, boxes, rank, bits)


def band_sum(backs, tables, t):
    total = None
    for k, back in enumerate(backs):
        term = back[:SUB, :] * tables[k, 0, t] - back[SUB:, :] * tables[k, 1, t]
        total = term if total is None else total + term
    return total


def energy_body(tables, *refs, samples):
    backs, out = refs[:-1], refs[-1]
    total = jnp.zeros((SUB, backs[0].shape[1]), F32)
    for t in range(samples):
        val = band_sum(backs, tables, t)
        total = total + val * val
    out[...] = jnp.broadcast_to(jnp.sum(total, axis=1, keepdims=True), out.shape)


def leaf_sum_body(src, out, slots, send, recv, *, n):
    me = lax.axis_index("leaf")

    def peer(d):
        got = me
        for bit in range(n.bit_length() - 1):
            if (d >> bit) & 1:
                got = got + (1 << bit) * (1 - 2 * (me // (1 << bit) % 2))
        return got

    barrier = pltpu.get_barrier_semaphore()
    for d in range(1, n):
        pl.semaphore_signal(
            barrier, inc=1, device_id={"leaf": peer(d)}, device_id_type=pl.DeviceIdType.MESH
        )
    pl.semaphore_wait(barrier, n - 1)
    copies = []
    for d in range(1, n):
        copy = pltpu.make_async_remote_copy(
            src_ref=src,
            dst_ref=slots.at[d],
            send_sem=send.at[d],
            recv_sem=recv.at[d],
            device_id={"leaf": peer(d)},
            device_id_type=pl.DeviceIdType.MESH,
        )
        copy.start()
        copies.append(copy)
    for copy in copies:
        copy.wait()
    total = src[...]
    for d in range(1, n):
        total = total + slots[d]
    out[...] = total


def leaf_sum(value, n, tag):
    vmem = pl.BlockSpec(memory_space=pltpu.VMEM)
    return pl.pallas_call(
        functools.partial(leaf_sum_body, n=n),
        out_shape=sds(value.shape),
        in_specs=[vmem],
        out_specs=vmem,
        scratch_shapes=[
            pltpu.VMEM((n,) + value.shape, F32),
            pltpu.SemaphoreType.DMA((n,)),
            pltpu.SemaphoreType.DMA((n,)),
        ],
        compiler_params=pltpu.CompilerParams(
            collective_id=tag, has_side_effects=True, vmem_limit_bytes=4 << 20
        ),
        cost_estimate=pl.CostEstimate(flops=1 << 20, bytes_accessed=1 << 16, transcendentals=0),
    )(value)


def amp_of(energy, scale, count):
    root = jnp.sqrt(energy[:, :1] / count + 1e-06)
    return scale[:, :1] * root


def next_levels(tables, own, energy, scale, hi, lo, *refs, samples, count, boxes, rank, bits, bands):
    backs, outs = refs[:bands], refs[bands:]
    amp = amp_of(energy, scale, count)
    inv = 1.0 / amp
    re = jnp.zeros((SUB, backs[0].shape[1]), F32)
    im = jnp.zeros((SUB, backs[0].shape[1]), F32)
    for t in range(samples):
        sig = jnp.clip(band_sum(backs, tables, t), -amp, amp) * inv
        re = re + sig * own[0, t]
        im = im - sig * own[1, t]
    forward_tail(jnp.concatenate([re, im], axis=0), hi, lo, outs, boxes, rank, bits)


def finish(tables, *refs, samples, count, halves, bands):
    energies = refs[:halves]
    scales = refs[halves : 2 * halves]
    backs = refs[2 * halves : 2 * halves + halves * bands]
    out = refs[-1]
    for h in range(halves):
        amp = amp_of(energies[h], scales[h], count)
        inv = 1.0 / amp
        for t in range(samples):
            sig = band_sum(backs[h * bands : (h + 1) * bands], tables, t)
            sig = jnp.clip(sig, -amp, amp) * inv
            out[t, h * SUB : (h + 1) * SUB, :] = sig


def cross_body(x, p, m, out):
    out[...] = dot2(x[...], m[0]) + dot2(p[...], m[1])


def back_first(*refs):
    xs, (m, keep, out) = refs[:-3], refs[-3:]
    v = xs[0][...]
    for x in xs[1:]:
        v = v + x[...]
    keep[...] = v
    out[...] = dot2(v, m[1])


def back_mid(x, inc, m, nxt, keep, out):
    v = dot2(x[...], m[0]) + inc[...]
    keep[...] = v
    out[...] = dot2(v, nxt[1])


def back_last(*refs, parts, boxes, rank, bits, final):
    xs, incs = refs[:parts], refs[parts : 2 * parts]
    m, hi, lo = refs[2 * parts : 2 * parts + 3]
    rest = refs[2 * parts + 3 :]
    v = jnp.concatenate(
        [dot2(xs[i][...], m[0]) + incs[i][...] for i in range(parts)], axis=0
    ).reshape(boxes, SUB, 2 * rank)
    v = local_levels_apply(v, hi, lo, reversed(range(bits)), bits)
    if final:
        idx, out, tmp = rest
    else:
        (out,) = rest
        tmp = out
    for c in range(boxes):
        cols = slice(c * rank, (c + 1) * rank)
        tmp[:SUB, cols] = v[c, :, :rank]
        tmp[SUB:, cols] = v[c, :, rank:]
    if final:
        permute_rows(tmp, idx, out)


def image_body(*refs, parts, boxes, rank):
    xs = refs[:parts]
    wt, w, rho, couple = refs[parts : parts + 4]
    outs = refs[parts + 4 : 2 * parts + 4]
    st, acc, pre, pim = refs[2 * parts + 4 :]
    step = pl.program_id(0)
    width = 2 * rank
    per = boxes // parts

    @pl.when(step == 0)
    def _():
        for i in range(parts):
            pre[...] = xs[i][:, :rank]
            pim[...] = xs[i][:, rank:]
            for s in range(SUB):
                re = pre[pl.ds(s, per, stride=SUB), :].astype(BF16)
                im = pim[pl.ds(s, per, stride=SUB), :].astype(BF16)
                at = s * width
                st[i * per : (i + 1) * per, at : at + rank] = re
                st[i * per : (i + 1) * per, at + rank : at + width] = im
                st[boxes + i * per : boxes + (i + 1) * per, at : at + rank] = -im
                st[boxes + i * per : boxes + (i + 1) * per, at + rank : at + width] = re
        acc[...] = jnp.zeros_like(acc)

    r = rho[...].astype(F32)
    pair = jnp.concatenate([r, r], axis=1)
    k = couple[...]
    wtb = wt[...]
    wb = w[...]
    for s in range(SUB):
        cols = slice(s * width, (s + 1) * width)
        field = mm(wtb, st[:, cols])
        scaled = (pair * field).astype(BF16)
        echo = (pair * (field + mm(scaled, k))).astype(BF16)
        acc[:, cols] += mm(wb, echo)

    @pl.when(step == pl.num_programs(0) - 1)
    def _():
        for i in range(parts):
            top = slice(i * per, (i + 1) * per)
            low = slice(boxes + i * per, boxes + (i + 1) * per)
            for s in range(SUB):
                at = s * width
                a_re, a_im = acc[top, at : at + rank], acc[top, at + rank : at + width]
                b_re, b_im = acc[low, at : at + rank], acc[low, at + rank : at + width]
                pre[pl.ds(s, per, stride=SUB), :] = a_re + b_im
                pim[pl.ds(s, per, stride=SUB), :] = a_im - b_re
            outs[i][:, :rank] = pre[...]
            outs[i][:, rank:] = pim[...]


def image_pass(xs, wt, w, rho, couple, seg):
    parts = len(xs)
    points, double = wt.shape
    boxes = double // 2
    rank = rho.shape[1]
    width = 2 * rank
    quarter = points // 4
    blk = math.gcd(quarter, 1024)
    first = seg[0] * quarter // blk
    steps = seg[1] * quarter // blk
    whole = pl.BlockSpec(memory_space=pltpu.VMEM)
    return call(
        functools.partial(image_body, parts=parts, boxes=boxes, rank=rank),
        [sds(xs[0].shape)] * parts,
        [*xs, wt, w, rho, couple],
        2 * steps * blk * SUB * width * 2 * (2 * double + width),
        grid=(steps,),
        mib=24,
        in_specs=[whole] * parts
        + [
            pl.BlockSpec((blk, double), lambda i: (i + first, 0)),
            pl.BlockSpec((double, blk), lambda i: (0, i + first)),
            pl.BlockSpec((blk, rank), lambda i: (i + first, 0)),
            whole,
        ],
        out_specs=[whole] * parts,
        scratch=[
            pltpu.VMEM((double, SUB * width), BF16),
            pltpu.VMEM((double, SUB * width), F32),
            pltpu.VMEM((xs[0].shape[0], rank), F32),
            pltpu.VMEM((xs[0].shape[0], rank), F32),
        ],
    )


def on_device(
    excitation,
    freq_index,
    elem_order,
    level_factors,
    image_weights,
    coupling,
    reflectivity,
    clip_level,
):
    shots, samples, elems = excitation.shape
    rank = coupling.shape[-1]
    boxes = elems // rank
    bits = boxes.bit_length() - 1
    levels = level_factors.shape[2]
    n_cross = levels - bits
    leafs = lax.axis_size("leaf")
    bands = lax.axis_size("band")
    band_bits = bands.bit_length() - 1
    halves = shots // SUB
    parts = PARTS
    width = 2 * rank
    rows = boxes * SUB
    count = float(samples * elems * leafs)

    (hi, lo, hit, lot), (cross, crosst) = prepare(level_factors[0, 0], bits)
    w = image_weights[0].reshape(2 * boxes, image_weights.shape[3])
    wt = w.T
    couple = block_form(coupling[0, 0], coupling[0, 1])
    order = elem_order[0]
    inverse = jnp.argsort(order)
    idx = order.reshape(boxes, rank)
    inv_idx = inverse.astype(jnp.int32).reshape(boxes, rank)

    steps = jnp.arange(samples, dtype=F32)
    angle = 2.0 * math.pi / samples * freq_index[0].astype(F32) * steps
    own = jnp.stack([jnp.cos(angle), jnp.sin(angle)])
    smem = pl.BlockSpec(memory_space=pltpu.SMEM)
    vmem = pl.BlockSpec(memory_space=pltpu.VMEM)

    def gather_bands(value):
        got = [value]
        for bit in reversed(range(band_bits)):
            got = got + [swap(v, "band", bit) for v in got]
        return got

    tables = jnp.stack(gather_bands(own))
    scale = (4.0 + clip_level.astype(F32)) / 10.0
    scales = [
        jnp.broadcast_to(scale[h * SUB : (h + 1) * SUB, None], (SUB, 128)) for h in range(halves)
    ]

    eye = jnp.eye(SUB, dtype=F32)
    half_mat = jnp.concatenate(
        [
            (eye[:, :, None] * own[0][None, None, :]).reshape(SUB, SUB * samples),
            (eye[:, :, None] * -own[1][None, None, :]).reshape(SUB, SUB * samples),
        ],
        axis=0,
    )
    flat_exc = excitation.reshape(shots * samples, elems)
    in_rows = SUB * samples
    specs = [
        call(
            first_spec,
            [sds((SUB * 2, elems))],
            [flat_exc, idx, half_mat],
            1 << 33,
            grid=(1,),
            in_specs=[pl.BlockSpec((in_rows, elems), lambda i, h=h: (h, 0)), vmem, vmem],
            scratch=[pltpu.VMEM((SUB * 2, elems), F32)],
            mib=20,
        )[0]
        for h in range(halves)
    ]
    part_out = [sds((rows // parts, width))] * parts
    loc_flops = 6 * rows * width * width * bits
    cr_flops = 8 * rows // parts * width * width
    xs = []
    for h in range(halves):
        xs.append(
            call(
                functools.partial(start_levels, boxes=boxes, rank=rank, bits=bits),
                part_out,
                [specs[h], hi, lo],
                loc_flops,
            )
        )
    result = None

    def back_level(state):
        x, sent, l, inc = state
        for i in range(parts):
            x[i], sent[i] = call(
                back_mid,
                part_out[:1] * 2,
                [x[i], inc[i], crosst[l], crosst[l - 1]],
                cr_flops,
                mib=6,
            )
        state[2] = l - 1

    for it in range(ITERS):
        final = it == ITERS - 1
        all_backs, all_energy = [], []
        held = {}
        for h in range(halves):
            x = list(xs[h])
            for l in range(n_cross):
                for i in range(parts):
                    p = swap(x[i], "leaf", l)
                    x[i] = call(cross_body, part_out[:1], [x[i], p, cross[l]], cr_flops, mib=6)[0]
            if it == 0 and h == 0:
                x, inv_idx = lax.optimization_barrier((x, inv_idx))
            segs = []
            for g, seg in enumerate(SEGS):
                if h > 0:
                    prev = held[h - 1]
                    x, prev[1] = lax.optimization_barrier((x, prev[1]))
                segs.append(image_pass(x, wt, w, reflectivity, couple, seg))
                if h > 0 and prev[2] > 0:
                    prev[3] = [swap(v, "leaf", prev[2]) for v in prev[1]]
                    segs[g], prev[3] = lax.optimization_barrier((segs[g], prev[3]))
                    back_level(prev)
            sent = [None] * parts
            for i in range(parts):
                x[i], sent[i] = call(
                    back_first,
                    part_out[:1] * 2,
                    [*[g[i] for g in segs], crosst[n_cross - 1]],
                    cr_flops // 2,
                    mib=6,
                )
            held[h] = [x, sent, n_cross - 1, None]
        for h in range(halves):
            state = held[h]
            while state[2] > 0:
                state[3] = [swap(v, "leaf", state[2]) for v in state[1]]
                if h > 0:
                    state[3], _ = lax.optimization_barrier((state[3], all_backs[h - 1][0]))
                back_level(state)
            x = state[0]
            inc = [swap(v, "leaf", 0) for v in state[1]]
            if h > 0:
                inc, _ = lax.optimization_barrier((inc, all_energy[h - 1]))
            back = call(
                functools.partial(
                    back_last, parts=parts, boxes=boxes, rank=rank, bits=bits, final=final
                ),
                [sds((2 * SUB, elems))],
                [*x, *inc, crosst[0], hit, lot] + ([inv_idx] if final else []),
                loc_flops,
                scratch=[pltpu.VMEM((2 * SUB, elems), F32)] if final else [],
            )[0]
            backs = gather_bands(back)
            energy = call(
                functools.partial(energy_body, samples=samples),
                [sds((SUB, 128))],
                [tables, *backs],
                1 << 22,
                in_specs=[smem] + [vmem] * bands,
            )[0]
            energy = leaf_sum(energy, leafs, it * halves + h)
            all_backs.append(backs)
            all_energy.append(energy)
        if not final:
            xs = [
                call(
                    functools.partial(
                        next_levels,
                        samples=samples,
                        count=count,
                        boxes=boxes,
                        rank=rank,
                        bits=bits,
                        bands=bands,
                    ),
                    part_out,
                    [tables, own, all_energy[h], scales[h], hi, lo, *all_backs[h]],
                    loc_flops,
                    in_specs=[smem, smem] + [vmem] * (4 + bands),
                )
                for h in range(halves)
            ]
        else:
            flat = [b for bs in all_backs for b in bs]
            result = call(
                functools.partial(finish, samples=samples, count=count, halves=halves, bands=bands),
                [sds((samples, shots, elems))],
                [tables, *all_energy, *scales, *flat],
                1 << 24,
                in_specs=[smem] + [vmem] * (2 * halves + len(flat)),
            )[0]
    return result.transpose(1, 0, 2)


def solution(mesh):
    return jax.shard_map(
        on_device,
        mesh=mesh,
        in_specs=(
            P(None, None, "leaf"),
            P("band"),
            P("leaf", None),
            P("band", "leaf", None, None, None, None, None),
            P("band", None, None, "leaf"),
            P("band", None, None, None),
            P("leaf", None),
            P(),
        ),
        out_specs=P(None, None, "leaf"),
        check_vma=False,
    )
```
